32 devices in a mesh: dp: 4 (over y, core), seq: 8 (over z, x).
Axes of the slice: x: 2, y: 2, z: 4, core: 2. Of those that a mesh axis runs over, the one named last changes fastest.
Arguments:
- tokens: bfloat16 [16, 2048, 768], P('dp', 'seq'), may hold values from -6 to 6
- segments: int32 [16, 2048], P('dp'), may hold values from 0 to 2, as said below
- live_blocks: int32 [16], P('dp'), may hold values from 16 to 32
- random_blocks: int32 [16, 32, 3], P('dp'), may hold values from 2 to 31, as said below
- w_query: bfloat16 [768, 768], P(('dp', 'seq')), may hold values from -0.21875 to 0.21875
- b_query: bfloat16 [768], P(('dp', 'seq')), may hold values from -3 to 3
- w_key: bfloat16 [768, 768], P(('dp', 'seq')), may hold values from -0.21875 to 0.21875
- w_value: bfloat16 [768, 768], P(('dp', 'seq')), may hold values from -0.21875 to 0.21875
- b_value: bfloat16 [768], P(('dp', 'seq')), may hold values from -3 to 3
- w_output: bfloat16 [768, 768], P(('dp', 'seq')), may hold values from -0.875 to 0.875
- b_output: bfloat16 [768], P(('dp', 'seq')), may hold values from -3 to 3
- g_first: bfloat16 [768], P(('dp', 'seq')), may hold values from 0.5 to 1.5
- b_first: bfloat16 [768], P(('dp', 'seq')), may hold values from -3 to 3
- w_hidden: bfloat16 [768, 3072], P(('dp', 'seq')), may hold values from -0.21875 to 0.21875
- b_hidden: bfloat16 [3072], P(('dp', 'seq')), may hold values from -3 to 3
- w_down: bfloat16 [3072, 768], P(('dp', 'seq')), may hold values from -0.109375 to 0.109375
- b_down: bfloat16 [768], P(('dp', 'seq')), may hold values from -3 to 3
- g_second: bfloat16 [768], P(('dp', 'seq')), may hold values from 0.5 to 1.5
- b_second: bfloat16 [768], P(('dp', 'seq')), may hold values from -3 to 3
- cotangent: bfloat16 [16, 2048, 768], P('dp', 'seq'), may hold values from -6 to 6
Outputs:
- result: bfloat16 [16, 2048, 768], P('dp', 'seq')
- token_grad: bfloat16 [16, 2048, 768], P('dp', 'seq')
- dw_query: float32 [768, 768], P(('dp', 'seq'))
- db_query: float32 [768], P(('dp', 'seq'))
- dw_key: float32 [768, 768], P(('dp', 'seq'))
- dw_value: float32 [768, 768], P(('dp', 'seq'))
- db_value: float32 [768], P(('dp', 'seq'))
- dw_output: float32 [768, 768], P(('dp', 'seq'))
- db_output: float32 [768], P(('dp', 'seq'))
- dg_first: float32 [768], P(('dp', 'seq'))
- db_first: float32 [768], P(('dp', 'seq'))
- dw_hidden: float32 [768, 3072], P(('dp', 'seq'))
- db_hidden: float32 [3072], P(('dp', 'seq'))
- down_weight_grad: float32 [3072, 768], P(('dp', 'seq'))
- db_down: float32 [768], P(('dp', 'seq'))
- dg_second: float32 [768], P(('dp', 'seq'))
- db_second: float32 [768], P(('dp', 'seq'))
The draws below stay inside these ranges and needn't reach their ends.
Inputs may be any that keep to these rules, and one draw needn't show every extreme that they name: `segments`: document numbers never fall along a sequence and each document is one run of tokens; document 0 holds the first 1536 tokens or more and ends at least 128 tokens before the sequence's end; documents 1 and 2 hold at least one token each. `random_blocks`: seen in groups of 4 consecutive query blocks: the 3 entries of a query block are distinct, none is 0 or 1, none lies in its own group or a group beside it, and the 12 entries of one group fall at most 3 times into any single group.
All inputs are finite; a program needn't handle non-finite values.
Results may differ from the reference program's by a relative error of at most 0.015.
Values may be sent and summed in bfloat16 or wider, within the bound.
No kernel may reach another device: no remote copies, remote signals or barrier semaphores. Data moves between devices by JAX's collectives and lax.ppermute only.
A program may use at most 384 MiB of HBM per device.

```python
import math
import jax
import jax.numpy as jnp
from jax import lax

D = 768
HEADS = 12
FF = 3072
BLOCK = 64
RAND = 3
BLK_DEV = 4
NB = 32
SEQ_LEN = 2048
SEQUENCES = 16


def draw_segments(key, part):
    key_first, key_second = jax.random.split(jax.random.fold_in(key, 29))
    first_end = jax.random.randint(key_first, (SEQUENCES, 1), 3 * SEQ_LEN // 4, SEQ_LEN - 2 * BLOCK + 1)
    offset_draw = jax.random.randint(key_second, (SEQUENCES, 1), 0, 1 << 20)
    second_end = first_end + 1 + offset_draw % (SEQ_LEN - first_end - 1)
    positions = jnp.arange(SEQ_LEN, dtype=jnp.int32)[None, :]
    segment_ids = (positions >= first_end).astype(jnp.int32) + (positions >= second_end).astype(jnp.int32)
    return segment_ids.astype(jnp.int32)


def draw_random_blocks(key, part):
    groups = NB // BLK_DEV
    pair_count = BLK_DEV * RAND
    key_order, key_inner = jax.random.split(jax.random.fold_in(key, 17))
    scores = jax.random.randint(key_order, (SEQUENCES, groups, groups), 0, 1 << 20)
    group_ids = jnp.arange(groups, dtype=jnp.int32)
    scores = scores * groups + group_ids[None, None, :]
    nearby = jnp.abs(group_ids[:, None] - group_ids[None, :]) <= 1
    scores = jnp.where(nearby[None], scores + (1 << 29), scores)
    ordering = jnp.argsort(scores, axis=-1, stable=True).astype(jnp.int32)
    available = groups - jnp.sum(nearby.astype(jnp.int32), axis=1)
    positions = jnp.arange(pair_count, dtype=jnp.int32)[None, :] % available[:, None]
    positions = jnp.broadcast_to(positions[None], (SEQUENCES, groups, pair_count))
    holders = jnp.take_along_axis(ordering, positions, axis=-1)
    raw_draw = jax.random.randint(key_inner, (SEQUENCES, groups, pair_count), 0, 1 << 20)
    within = jnp.where(holders == 0, 2 + raw_draw % (BLK_DEV - 2), raw_draw % BLK_DEV)
    table = holders * BLK_DEV + within
    return table.reshape(SEQUENCES, NB, RAND).astype(jnp.int32)


def set_ends(array, stream_key, low, high):
    dims = array.shape
    spot = [jax.random.randint(jax.random.fold_in(stream_key, axis), (), 0, dims[axis]) for axis in range(len(dims))]
    array = array.at[tuple(spot)].set(low)
    longest = dims.index(max(dims))
    spot[longest] = (spot[longest] + 1) % dims[longest]
    return array.at[tuple(spot)].set(high)


def shard_levels(stream_key, extent, pieces, least, largest):
    loudness, own = 1.0, jax.random.fold_in(stream_key, 6)
    for axis_at, shards_of in pieces:
        steps = jnp.exp(jax.random.uniform(jax.random.fold_in(own, axis_at), (shards_of,), jnp.float32, least / len(pieces), largest / len(pieces)))
        loudness = loudness * jnp.repeat(steps, extent[axis_at] // shards_of).reshape([-1 if axis == axis_at else 1 for axis in range(len(extent))])
    return loudness


def normal_values(own_key, dims, deviation, reach, cuts=(), kind=jnp.bfloat16):
    values = jax.random.normal(own_key, dims, jnp.float32) * deviation
    if len(cuts) > 0:
        values = shard_levels(own_key, dims, cuts, -0.22, 0.18) * values
    return jnp.clip(values, min=-reach, max=reach).astype(kind)


def setup_inputs(seed: int = 0) -> dict:
    splits = jax.random.split(jax.random.key(seed), 21)
    tokens = normal_values(splits[0], (SEQUENCES, SEQ_LEN, D), 1.0, 6.0, ((0, 4), (1, 8)))
    segments = draw_segments(jax.random.fold_in(splits[20], 71), 0)
    live_blocks = set_ends(jax.random.randint(splits[2], (SEQUENCES,), NB // 2, NB + 1), jax.random.fold_in(splits[2], 1), NB // 2, NB).astype(jnp.int32)
    random_blocks = draw_random_blocks(jax.random.fold_in(splits[20], 71), 0)
    w_query = normal_values(splits[4], (D, D), D ** -0.5, 0.21875, ((0, 32),))
    b_query = normal_values(splits[5], (D,), 0.3, 3.0, ((0, 32),))
    w_key = normal_values(splits[6], (D, D), D ** -0.5, 0.21875, ((0, 32),))
    w_value = normal_values(splits[7], (D, D), D ** -0.5, 0.21875, ((0, 32),))
    b_value = normal_values(splits[8], (D,), 0.3, 3.0, ((0, 32),))
    w_output = normal_values(splits[9], (D, D), (D // 16) ** -0.5, 0.875, ((0, 32),))
    b_output = normal_values(splits[10], (D,), 0.3, 3.0, ((0, 32),))
    g_first = jnp.clip(1.0 + 0.1 * jax.random.normal(splits[11], (D,), jnp.float32), 0.5, 1.5).astype(jnp.bfloat16)
    b_first = normal_values(splits[12], (D,), 0.3, 3.0, ((0, 32),))
    w_hidden = normal_values(splits[13], (D, FF), D ** -0.5, 0.21875, ((0, 32),))
    b_hidden = normal_values(splits[14], (FF,), 0.3, 3.0, ((0, 32),))
    w_down = normal_values(splits[15], (FF, D), FF ** -0.5, 0.109375, ((0, 32),))
    b_down = normal_values(splits[16], (D,), 0.3, 3.0, ((0, 32),))
    g_second = jnp.clip(1.0 + 0.1 * jax.random.normal(splits[17], (D,), jnp.float32), 0.5, 1.5).astype(jnp.bfloat16)
    b_second = normal_values(splits[18], (D,), 0.3, 3.0, ((0, 32),))
    cotangent = normal_values(splits[19], (SEQUENCES, SEQ_LEN, D), 1.0, 6.0, ((0, 4), (1, 8)))
    return {"tokens": tokens, "segments": segments, "live_blocks": live_blocks, "random_blocks": random_blocks, "w_query": w_query, "b_query": b_query, "w_key": w_key, "w_value": w_value, "b_value": b_value, "w_output": w_output, "b_output": b_output, "g_first": g_first, "b_first": b_first, "w_hidden": w_hidden, "b_hidden": b_hidden, "w_down": w_down, "b_down": b_down, "g_second": g_second, "b_second": b_second, "cotangent": cotangent}


EPS = 1e-06
NEG = -1e+30

@jax.custom_vjp
def low(v):
    return lax.optimization_barrier(v.astype(jnp.bfloat16)).astype(jnp.float32)

@jax.custom_vjp
def low_back(v):
    return v

def low_keep(v):
    return (low(v), None)

def low_pass(kept, grad):
    return (grad,)

def back_keep(v):
    return (v, None)

def back_low(kept, grad):
    return (low(grad),)
low.defvjp(low_keep, low_pass)
low_back.defvjp(back_keep, back_low)

def matmul(rows_on_left, right_cols):
    return jnp.dot(rows_on_left, right_cols, precision=lax.Precision.HIGHEST)

def layer_norm(residual, gains, offset):
    average = lax.optimization_barrier(jnp.mean(residual, axis=-1, keepdims=True))
    centred = residual - average
    inv_std = lax.rsqrt(lax.optimization_barrier(jnp.mean(centred * centred, axis=-1, keepdims=True)) + EPS)
    return centred * inv_std * gains + offset

def sparse_attention(query, keys, values, segment_row, live, table):
    length_total, width = query.shape
    head_size = width // HEADS
    scale = head_size ** (-0.5)
    total_blocks = length_total // BLOCK
    lead = 2 * BLOCK
    group = math.gcd(total_blocks, max(1, 512 // BLOCK))
    query_heads = query.reshape(length_total, HEADS, head_size)
    key_heads = keys.reshape(length_total, HEADS, head_size)
    value_heads = values.reshape(length_total, HEADS, head_size)
    within = jnp.arange(BLOCK, dtype=jnp.int32)

    def regular(index_of_group):
        block_ids = index_of_group * group + jnp.arange(group, dtype=jnp.int32)
        window_ids = block_ids[:, None] + jnp.arange(-1, 2, dtype=jnp.int32)[None, :]
        window_ok = (window_ids >= 2) & (window_ids < total_blocks)
        global_ids = jnp.broadcast_to(jnp.arange(2, dtype=jnp.int32)[None, :], (group, 2))
        random_ids = jnp.take(table, block_ids, axis=0).astype(jnp.int32)
        slot_ids = jnp.concatenate([window_ids, global_ids, random_ids], axis=1)
        slot_ok = jnp.concatenate([window_ok, jnp.ones((group, 2 + RAND), dtype=bool)], axis=1)
        slot_ok = slot_ok & (slot_ids < live)
        key_pos = (jnp.clip(slot_ids, 0, total_blocks - 1)[:, :, None] * BLOCK + within).reshape(group, -1)
        key_ok = jnp.repeat(slot_ok, BLOCK, axis=1)
        query_pos = block_ids[:, None] * BLOCK + within[None, :]
        key_seg = jnp.take(segment_row, key_pos)
        query_seg = jnp.take(segment_row, query_pos)
        query_live = block_ids < live
        allowed = key_ok[:, None, :] & (query_seg[:, :, None] == key_seg[:, None, :]) & query_live[:, None, None]
        picked_keys = jnp.take(key_heads, key_pos, axis=0)
        picked_values = jnp.take(value_heads, key_pos, axis=0)
        picked_query = jnp.take(query_heads, query_pos, axis=0)
        scores = low_back(jnp.einsum('gbhd,gkhd->ghbk', picked_query, picked_keys, precision=lax.Precision.HIGHEST) * scale)
        mask_four = allowed[:, None]
        peak = lax.optimization_barrier(jnp.max(jnp.where(mask_four, scores, NEG), axis=-1, keepdims=True))
        expo = jnp.where(mask_four, jnp.exp(jnp.where(mask_four, scores - peak, NEG)), 0.0)
        dead = 1.0 - query_live.astype(jnp.float32)[:, None, None, None]
        probs = low(expo / (lax.optimization_barrier(jnp.sum(expo, axis=-1, keepdims=True)) + dead))
        attended = jnp.einsum('ghbk,gkhd->gbhd', probs, picked_values, precision=lax.Precision.HIGHEST)
        return attended.reshape(group * BLOCK, width)
    regular_out = lax.map(jax.checkpoint(regular), jnp.arange(total_blocks // group, dtype=jnp.int32))
    regular_out = regular_out.reshape(length_total, width)
    key_live = jnp.arange(length_total, dtype=jnp.int32) // BLOCK < live
    global_mask = (segment_row[:lead, None] == segment_row[None, :]) & key_live[None, :]

    def global_rows(lead_query):
        scores = low_back(jnp.einsum('qhd,khd->hqk', lead_query, key_heads, precision=lax.Precision.HIGHEST) * scale)
        mask_three = global_mask[None]
        peak = lax.optimization_barrier(jnp.max(jnp.where(mask_three, scores, NEG), axis=-1, keepdims=True))
        expo = jnp.where(mask_three, jnp.exp(jnp.where(mask_three, scores - peak, NEG)), 0.0)
        probs = low(expo / lax.optimization_barrier(jnp.sum(expo, axis=-1, keepdims=True)))
        attended = jnp.einsum('hqk,khd->qhd', probs, value_heads, precision=lax.Precision.HIGHEST)
        return attended.reshape(lead, width)
    global_out = jax.checkpoint(global_rows)(query_heads[:lead])
    return jnp.concatenate([global_out, regular_out[lead:]], axis=0)

def layer(params, tokens_f, segment_row, live, table):
    w_query, b_query, w_key, w_value, b_value, w_output, b_output, g_first, b_first, w_hidden, b_hidden, w_down, b_down, g_second, b_second = params
    query = low_back(low(matmul(tokens_f, w_query) + b_query))
    keys = low_back(low(matmul(tokens_f, w_key)))
    values = low_back(low(matmul(tokens_f, w_value) + b_value))
    attended = low_back(low(sparse_attention(query, keys, values, segment_row, live, table)))
    attn_sum = low_back(matmul(attended, w_output) + b_output)
    first = layer_norm(tokens_f + attn_sum, g_first, b_first)
    pre_act = low_back(matmul(low(first), w_hidden) + b_hidden)
    activ = low(jax.nn.gelu(pre_act, approximate=True))
    branch = low_back(matmul(activ, w_down) + b_down)
    return layer_norm(first + branch, g_second, b_second)

def reference(tokens, segments, live_blocks, random_blocks, w_query, b_query, w_key, w_value, b_value, w_output, b_output, g_first, b_first, w_hidden, b_hidden, w_down, b_down, g_second, b_second, cotangent):
    params = tuple((weight_matrix.astype(jnp.float32) for weight_matrix in (w_query, b_query, w_key, w_value, b_value, w_output, b_output, g_first, b_first, w_hidden, b_hidden, w_down, b_down, g_second, b_second)))

    def one_sequence(totals, items):
        tokens_row, segment_row, live, table, cot_row = items

        def apply(weights, inputs):
            return layer(weights, inputs, segment_row, live, table)
        output, pull = jax.vjp(apply, params, tokens_row.astype(jnp.float32))
        grad_params, grad_tokens = pull(cot_row.astype(jnp.float32))
        totals = tuple((left + right for left, right in zip(totals, grad_params)))
        return (totals, (output.astype(jnp.bfloat16), grad_tokens.astype(jnp.bfloat16)))
    start = tuple((jnp.zeros(weight_matrix.shape, jnp.float32) for weight_matrix in params))
    totals, (results, token_grads) = lax.scan(one_sequence, start, (tokens, segments, live_blocks, random_blocks, cotangent))
    return (results, token_grads, totals[0], totals[1], totals[2], totals[3], totals[4], totals[5], totals[6], totals[7], totals[8], totals[9], totals[10], totals[11], totals[12], totals[13], totals[14])
```

```python
import functools

import jax
import jax.numpy as jnp
from jax import lax
from jax.experimental import pallas as pl
from jax.experimental.pallas import tpu as pltpu
from jax.sharding import PartitionSpec as P

HEADS = 12
RAND = 3
BLOCK = 64
EPS = 1e-06
SLOTS = 8
NEG = -1e30
F32 = jnp.float32
BF = jnp.bfloat16


def contract(a, b, da, db):
    return lax.dot_general(a, b, (((da,), (db,)), ((), ())), preferred_element_type=F32)


def block_rows(place):
    return pl.ds(pl.multiple_of(place * BLOCK, BLOCK), BLOCK)


def two_heads(rows):
    left = lax.broadcasted_iota(jnp.int32, rows.shape, 1) < BLOCK
    zero = jnp.zeros_like(rows)
    return jnp.concatenate([jnp.where(left, rows, zero), jnp.where(left, zero, rows)], axis=0)


def own_halves(square):
    left = lax.broadcasted_iota(jnp.int32, (BLOCK, 2 * BLOCK), 1) < BLOCK
    return jnp.where(left, square[:BLOCK], square[BLOCK:])


def pair_lanes(base, pair):
    return pl.ds(base + pair * 2 * BLOCK, 2 * BLOCK)


def slot_bias(slots_ref, segcol_ref, query_seg, block):
    parts = []
    for slot in range(SLOTS):
        seg = segcol_ref[block_rows(slots_ref[block, slot]), :]
        if slot < 3:
            seg = jnp.where(slots_ref[block, SLOTS + 1 + slot] > 0, seg, -1)
        parts.append(seg)
    return jnp.where(jnp.concatenate(parts, axis=0) == query_seg, 0.0, NEG)


def slot_rows(slots_ref, ref, block, lanes):
    return jnp.concatenate(
        [ref[block_rows(slots_ref[block, slot]), lanes] for slot in range(SLOTS)], axis=0
    )


def attention_forward_kernel(
    pairs, slots_ref, live_ref, qkv_ref, segcol_ref, segrow_ref, out_ref, log_ref, held
):
    width = pairs * 2 * BLOCK
    total = qkv_ref.shape[0]
    blocks = total // BLOCK
    chunk = SLOTS * BLOCK
    scale = BLOCK ** (-0.5)

    def regular(block, carry):
        place = slots_ref[block, SLOTS]

        @pl.when(block < live_ref[0])
        def _():
            bias = slot_bias(slots_ref, segcol_ref, segrow_ref[place], block)
            for pair in range(pairs):
                query = two_heads(qkv_ref[block_rows(place), pair_lanes(0, pair)] * scale)
                keys = slot_rows(slots_ref, qkv_ref, block, pair_lanes(width, pair))
                values = slot_rows(slots_ref, qkv_ref, block, pair_lanes(2 * width, pair))
                scores = contract(keys, query, 1, 1) + bias
                peak = jnp.max(scores, axis=0, keepdims=True)
                expo = jnp.exp(scores - peak)
                denom = jnp.sum(expo, axis=0, keepdims=True)
                probs = (expo * (1.0 / denom)).astype(BF)
                out = own_halves(contract(probs, values, 0, 0))
                out_ref[block_rows(place), pair_lanes(0, pair)] = out.astype(BF)
                log_ref[place, :, pair_lanes(0, pair)] = peak + jnp.log(denom)

        @pl.when(block >= live_ref[0])
        def _():
            out_ref[block_rows(place), :] = jnp.zeros((BLOCK, width), BF)
            log_ref[place] = jnp.zeros((1, width), F32)

        return carry

    lax.fori_loop(2, blocks, regular, 0)

    def leading(block, carry):
        place = slots_ref[block, SLOTS]
        query_seg = segrow_ref[place]
        for pair in range(pairs):
            query = two_heads(qkv_ref[block_rows(place), pair_lanes(0, pair)] * scale)
            peak = jnp.full((1, 2 * BLOCK), NEG, F32)
            for start in range(0, total, chunk):
                bias = jnp.where(segcol_ref[pl.ds(start, chunk), :] == query_seg, 0.0, NEG)
                keys = qkv_ref[pl.ds(start, chunk), pair_lanes(width, pair)]
                scores = contract(keys, query, 1, 1) + bias
                held[pl.ds(start, chunk), :] = scores
                peak = jnp.maximum(peak, jnp.max(scores, axis=0, keepdims=True))
            denom = jnp.zeros((1, 2 * BLOCK), F32)
            for start in range(0, total, chunk):
                expo = jnp.exp(held[pl.ds(start, chunk), :] - peak)
                held[pl.ds(start, chunk), :] = expo
                denom = denom + jnp.sum(expo, axis=0, keepdims=True)
            inverse = 1.0 / denom
            out = jnp.zeros((2 * BLOCK, 2 * BLOCK), F32)
            for start in range(0, total, chunk):
                probs = (held[pl.ds(start, chunk), :] * inverse).astype(BF)
                values = qkv_ref[pl.ds(start, chunk), pair_lanes(2 * width, pair)]
                out = out + contract(probs, values, 0, 0)
            out_ref[block_rows(place), pair_lanes(0, pair)] = own_halves(out).astype(BF)
            log_ref[place, :, pair_lanes(0, pair)] = peak + jnp.log(denom)
        return carry

    lax.fori_loop(0, 2, leading, 0)


def attention_backward_kernel(
    pairs, slots_ref, live_ref, qkv_ref, grad_ref, log_ref, segcol_ref, segrow_ref,
    out_ref, key_sum, value_sum, held, held_grad
):
    width = pairs * 2 * BLOCK
    total = qkv_ref.shape[0]
    blocks = total // BLOCK
    chunk = SLOTS * BLOCK
    scale = BLOCK ** (-0.5)

    def clear(step, carry):
        here = pl.ds(pl.multiple_of(step * BLOCK, BLOCK), BLOCK)
        key_sum[here, :] = jnp.zeros((BLOCK, width), F32)
        value_sum[here, :] = jnp.zeros((BLOCK, width), F32)
        return carry

    lax.fori_loop(0, blocks, clear, 0)

    def regular(block, carry):
        place = slots_ref[block, SLOTS]

        @pl.when(block < live_ref[0])
        def _():
            bias = slot_bias(slots_ref, segcol_ref, segrow_ref[place], block)
            for pair in range(pairs):
                query = two_heads(qkv_ref[block_rows(place), pair_lanes(0, pair)] * scale)
                grad = two_heads(grad_ref[block_rows(place), pair_lanes(0, pair)])
                keys = slot_rows(slots_ref, qkv_ref, block, pair_lanes(width, pair))
                values = slot_rows(slots_ref, qkv_ref, block, pair_lanes(2 * width, pair))
                scores = contract(keys, query, 1, 1) + bias
                probs = jnp.exp(scores - log_ref[place, :, pair_lanes(0, pair)])
                grad_probs = contract(values, grad, 1, 1)
                delta = jnp.sum(probs * grad_probs, axis=0, keepdims=True)
                grad_scores = (probs * (grad_probs - delta)).astype(BF)
                grad_query = own_halves(contract(grad_scores, keys, 0, 0)) * scale
                out_ref[block_rows(place), pair_lanes(0, pair)] = grad_query.astype(BF)
                grad_keys = contract(grad_scores, query, 1, 0)
                grad_values = contract(probs.astype(BF), grad, 1, 0)
                for slot in range(SLOTS):
                    here = block_rows(slots_ref[block, slot])
                    part = slice(slot * BLOCK, (slot + 1) * BLOCK)
                    key_sum[here, pair_lanes(0, pair)] += grad_keys[part]
                    value_sum[here, pair_lanes(0, pair)] += grad_values[part]

        @pl.when(block >= live_ref[0])
        def _():
            out_ref[block_rows(place), pl.ds(0, width)] = jnp.zeros((BLOCK, width), BF)

        return carry

    lax.fori_loop(2, blocks, regular, 0)

    def leading(block, carry):
        place = slots_ref[block, SLOTS]
        query_seg = segrow_ref[place]
        for pair in range(pairs):
            query = two_heads(qkv_ref[block_rows(place), pair_lanes(0, pair)] * scale)
            grad = two_heads(grad_ref[block_rows(place), pair_lanes(0, pair)])
            log_total = log_ref[place, :, pair_lanes(0, pair)]
            delta = jnp.zeros((1, 2 * BLOCK), F32)
            for start in range(0, total, chunk):
                here = pl.ds(start, chunk)
                bias = jnp.where(segcol_ref[here, :] == query_seg, 0.0, NEG)
                scores = contract(qkv_ref[here, pair_lanes(width, pair)], query, 1, 1) + bias
                probs = jnp.exp(scores - log_total)
                grad_probs = contract(qkv_ref[here, pair_lanes(2 * width, pair)], grad, 1, 1)
                held[here, :] = probs
                held_grad[here, :] = grad_probs
                delta = delta + jnp.sum(probs * grad_probs, axis=0, keepdims=True)
            grad_query = jnp.zeros((2 * BLOCK, 2 * BLOCK), F32)
            for start in range(0, total, chunk):
                here = pl.ds(start, chunk)
                probs = held[here, :]
                grad_scores = (probs * (held_grad[here, :] - delta)).astype(BF)
                keys = qkv_ref[here, pair_lanes(width, pair)]
                grad_query = grad_query + contract(grad_scores, keys, 0, 0)
                key_sum[here, pair_lanes(0, pair)] += contract(grad_scores, query, 1, 0)
                value_sum[here, pair_lanes(0, pair)] += contract(probs.astype(BF), grad, 1, 0)
            grad_query = own_halves(grad_query) * scale
            out_ref[block_rows(place), pair_lanes(0, pair)] = grad_query.astype(BF)
        return carry

    lax.fori_loop(0, 2, leading, 0)

    def finish(step, carry):
        here = pl.ds(pl.multiple_of(step * BLOCK, BLOCK), BLOCK)
        out_ref[here, pl.ds(width, width)] = key_sum[here, :].astype(BF)
        out_ref[here, pl.ds(2 * width, width)] = value_sum[here, :].astype(BF)
        return carry

    lax.fori_loop(0, blocks, finish, 0)


def attention_forward(slots, live, qkv, segcol, segrow):
    total, pairs = qkv.shape[0], qkv.shape[1] // (6 * BLOCK)
    width = pairs * 2 * BLOCK
    smem, vmem = pl.BlockSpec(memory_space=pltpu.SMEM), pl.BlockSpec(memory_space=pltpu.VMEM)
    return pl.pallas_call(
        functools.partial(attention_forward_kernel, pairs),
        out_shape=(
            jax.ShapeDtypeStruct((total, width), BF),
            jax.ShapeDtypeStruct((total // BLOCK, 1, width), F32),
        ),
        in_specs=[smem, smem, vmem, vmem, vmem],
        out_specs=(vmem, vmem),
        scratch_shapes=[pltpu.VMEM((total, 2 * BLOCK), F32)],
        compiler_params=pltpu.CompilerParams(vmem_limit_bytes=40 << 20),
        name="attention_forward",
    )(slots, live, qkv, segcol, segrow)


def attention_backward(slots, live, qkv, grad, log_total, segcol, segrow):
    total, pairs = qkv.shape[0], qkv.shape[1] // (6 * BLOCK)
    width = pairs * 2 * BLOCK
    smem, vmem = pl.BlockSpec(memory_space=pltpu.SMEM), pl.BlockSpec(memory_space=pltpu.VMEM)
    return pl.pallas_call(
        functools.partial(attention_backward_kernel, pairs),
        out_shape=jax.ShapeDtypeStruct((total, 3 * width), BF),
        in_specs=[smem, smem, vmem, vmem, vmem, vmem, vmem],
        out_specs=vmem,
        scratch_shapes=[
            pltpu.VMEM((total, width), F32),
            pltpu.VMEM((total, width), F32),
            pltpu.VMEM((total, 2 * BLOCK), F32),
            pltpu.VMEM((total, 2 * BLOCK), F32),
        ],
        compiler_params=pltpu.CompilerParams(vmem_limit_bytes=48 << 20),
        name="attention_backward",
    )(slots, live, qkv, grad, log_total, segcol, segrow)


def swap(array, bit):
    if bit == 0:
        count = lax.axis_size("dp")
        return lax.ppermute(array, "dp", [(i, i ^ 1) for i in range(count)])
    count = lax.axis_size("seq")
    return lax.ppermute(array, "seq", [(i, i ^ (1 << (bit - 1))) for i in range(count)])


def spread(array, team):
    array = array[None]
    bit = 0
    while (1 << bit) < team:
        array = jnp.concatenate([array, swap(array, bit)], axis=0)
        bit += 1
    return array


def hand_out(array, team):
    bit = team.bit_length() - 2
    kept = array
    parts = []
    for step in range(team):
        part = array[step]
        for bit in range(team.bit_length() - 1):
            if step >> bit & 1:
                part = swap(part, bit)
        parts.append(part)
    return parts


def from_rank(array, rank):
    team = array.shape[0]
    return jnp.stack([lax.dynamic_index_in_dim(array, rank ^ j, 0, False) for j in range(team)])


def to_plane(array, hold, sub, team, core):
    local, rows, width = array.shape
    part = rows // team
    view = array.reshape(local, sub, 2, part, width)
    mine = lax.dynamic_index_in_dim(view, core, 2, False)
    other = lax.dynamic_index_in_dim(view, 1 - core, 2, False)
    came = swap(other, 0)
    first = core == 0
    both = jnp.stack([jnp.where(first, mine, came), jnp.where(first, came, mine)])
    sent = both.reshape(hold * sub, part, width)
    return lax.all_to_all(sent, "seq", 0, 0, tiled=True).reshape(-1, width)


def from_plane(array, local, sub, team, core):
    width = array.shape[-1]
    groups = lax.axis_size("seq")
    got = lax.all_to_all(array.reshape(groups, -1, width), "seq", 0, 0, tiled=True)
    part = got.shape[1]
    both = got.reshape(2, local, sub, part, width)
    mine = lax.dynamic_index_in_dim(both, core, 0, False)
    other = lax.dynamic_index_in_dim(both, 1 - core, 0, False)
    came = swap(other, 0)
    first = core == 0
    whole = jnp.stack([jnp.where(first, mine, came), jnp.where(first, came, mine)], axis=2)
    return whole.reshape(local, sub * 2 * part, width)


def dot(a, b):
    return jnp.dot(a, b, preferred_element_type=F32)


def dot_t(a, b):
    return lax.dot_general(a, b, (((1,), (1,)), ((), ())), preferred_element_type=F32)


def t_dot(a, b):
    return lax.dot_general(a, b, (((0,), (0,)), ((), ())), preferred_element_type=F32)


def norm_forward(residual, gains, offset):
    average = jnp.mean(residual, axis=-1, keepdims=True)
    centred = residual - average
    inv_std = lax.rsqrt(jnp.mean(centred * centred, axis=-1, keepdims=True) + EPS)
    normed = centred * inv_std
    return (normed * gains + offset, normed, inv_std)


def norm_backward(grad_out, normed, inv_std, gains):
    scaled = grad_out * gains
    bracket = (
        scaled
        - jnp.mean(scaled, axis=-1, keepdims=True)
        - normed * jnp.mean(scaled * normed, axis=-1, keepdims=True)
    )
    return (inv_std * bracket, jnp.sum(grad_out * normed, axis=0), jnp.sum(grad_out, axis=0))


def gelu_tanh(values):
    return jax.nn.gelu(values, approximate=True)


def placing(seg, live, table, blocks, groups, team, rank):
    total = seg.shape[0]
    own = total // groups
    part = own // team
    token = jnp.arange(total, dtype=jnp.int32)

    def placed(row):
        by_part = row.reshape(groups, team, part).transpose(1, 0, 2)
        return from_rank(by_part, rank).reshape(total)

    seg_placed = jnp.where(placed(token) // BLOCK < live, placed(seg), -1)
    ids = jnp.arange(blocks, dtype=jnp.int32)

    def place_of(block):
        start = block * BLOCK
        group, inside = start // own, start % own
        return ((inside // part ^ rank) * (groups * part) + group * part + inside % part) // BLOCK

    window = ids[:, None] + jnp.arange(-1, 2, dtype=jnp.int32)[None, :]
    fits = ((window >= 2) & (window < blocks)).astype(jnp.int32)
    lead = jnp.broadcast_to(jnp.arange(2, dtype=jnp.int32)[None], (blocks, 2))
    keys = jnp.concatenate([jnp.clip(window, 0, blocks - 1), lead, table], axis=1)
    slots = jnp.concatenate([place_of(keys), place_of(ids)[:, None], fits], axis=1)
    segcol = jnp.broadcast_to(seg_placed[:, None], (total, 2 * BLOCK))
    half = seg_placed.reshape(blocks, 1, BLOCK)
    return slots, segcol, jnp.concatenate([half, half], axis=2)


def per_device(
    tokens,
    segments,
    live_blocks,
    random_blocks,
    w_query,
    b_query,
    w_key,
    w_value,
    b_value,
    w_output,
    b_output,
    g_first,
    b_first,
    w_hidden,
    b_hidden,
    w_down,
    b_down,
    g_second,
    b_second,
    cotangent,
):
    groups, fleet = lax.axis_size("seq"), lax.axis_size("dp") * lax.axis_size("seq")
    local, own, width = tokens.shape
    hidden = w_hidden.shape[1]
    total = segments.shape[1]
    blocks = random_blocks.shape[1]
    hold = 2 * local
    sub = groups // hold
    team = 2 * sub
    seq_at, core = lax.axis_index("seq"), lax.axis_index("dp") % 2
    rank = seq_at % sub * 2 + core
    heads = HEADS // team
    head_size = width // HEADS
    real = heads * head_size
    lanes = -(-real // (2 * BLOCK)) * 2 * BLOCK
    share = width // fleet
    share_hidden = hidden // fleet

    packed = jnp.concatenate(
        [
            segments,
            random_blocks.reshape(local, -1),
            live_blocks[:, None],
        ],
        axis=1,
    )
    other = swap(packed, 0)
    mine_at = seq_at // sub
    info = jnp.where(mine_at // local == core, packed, other)
    info = lax.dynamic_index_in_dim(info, mine_at % local, 0, False)
    seg, live = info[:total], info[total + blocks * RAND]
    table = info[total : total + blocks * RAND].reshape(blocks, RAND)
    slots, segcol, segrow = placing(seg, live, table, blocks, groups, team, rank)
    live = live[None]

    own_tokens = to_plane(tokens, hold, sub, team, core)
    all_tokens = spread(own_tokens, team).reshape(total, width)

    small = jnp.concatenate(
        [b_query, b_value, b_output, g_first, b_first, b_down, g_second, b_second, b_hidden]
    )
    small = jnp.pad(small, (0, 8 * width - small.shape[0])).reshape(8, width)
    first_parts = jnp.concatenate([w_query, w_key, w_value, small], axis=0)
    first_parts = lax.all_gather(first_parts, ("dp", "seq"), axis=0)
    dense_parts = jnp.concatenate([w_output, w_hidden.reshape(-1, width), w_down], axis=0)
    dense_parts = lax.all_gather(dense_parts, ("dp", "seq"), axis=0)

    def columns(matrix):
        piece = lax.dynamic_slice_in_dim(matrix, rank * real, real, matrix.ndim - 1)
        return jnp.pad(piece, [(0, 0)] * (matrix.ndim - 1) + [(0, lanes - real)])

    weights = [
        columns(first_parts[:, i * share : (i + 1) * share].reshape(width, width)) for i in range(3)
    ]
    w_qkv = jnp.concatenate(weights, axis=1)
    small = first_parts[:, 3 * share].astype(F32)
    vectors = [small[:, i * share : (i + 1) * share].reshape(width) for i in range(8)]
    b_query, b_value, b_output, g_first, b_first, b_down, g_second, b_second = vectors
    b_hidden = small[:, 8 * share : 8 * share + share_hidden].reshape(hidden)
    b_qkv = jnp.concatenate([columns(b_query), jnp.zeros((lanes,), F32), columns(b_value)])
    cut = share + share * hidden // width
    w_output = from_rank(dense_parts[:, :share].reshape(team, real, width), rank)
    w_output = w_output.reshape(width, width)
    w_hidden = dense_parts[:, share:cut].reshape(width, hidden)
    w_down = dense_parts[:, cut:].reshape(hidden, width)

    qkv = (dot(all_tokens, w_qkv) + b_qkv).astype(BF)
    attended, log_total = attention_forward(slots, live, qkv, segcol, segrow)
    attended = hand_out(attended.reshape(team, -1, lanes), team)
    attended = jnp.concatenate([part[:, :real] for part in attended], axis=1)

    first, n_first, inv_first = norm_forward(
        own_tokens.astype(F32) + (dot(attended, w_output) + b_output), g_first, b_first
    )
    hidden_in = first.astype(BF)
    pre_act = dot(hidden_in, w_hidden) + b_hidden
    activ = gelu_tanh(pre_act).astype(BF)
    result, n_second, inv_second = norm_forward(
        first + (dot(activ, w_down) + b_down), g_second, b_second
    )
    result = from_plane(result.astype(BF), local, sub, team, core)

    cot = to_plane(cotangent, hold, sub, team, core).astype(F32)
    grad_mid, dg_second, db_second = norm_backward(cot, n_second, inv_second, g_second)
    grad_branch = grad_mid.astype(BF)
    dw_down = t_dot(activ, grad_branch)
    db_down = jnp.sum(grad_branch.astype(F32), axis=0)
    unused, gelu_pull = jax.vjp(gelu_tanh, pre_act)
    grad_pre = gelu_pull(dot_t(grad_branch, w_down))[0].astype(BF)
    dw_hidden = t_dot(hidden_in, grad_pre)
    db_hidden = jnp.sum(grad_pre.astype(F32), axis=0)
    grad_first = grad_mid + dot_t(grad_pre, w_hidden)
    grad_resid, dg_first, db_first = norm_backward(grad_first, n_first, inv_first, g_first)
    grad_attn = grad_resid.astype(BF)
    dw_output = t_dot(attended, grad_attn)
    dw_output = from_rank(dw_output.reshape(team, real, width), rank).reshape(width, width)
    db_output = jnp.sum(grad_attn.astype(F32), axis=0)
    dense_grads = jnp.concatenate(
        [
            dw_output.astype(BF).reshape(fleet, share, width),
            dw_hidden.astype(BF).reshape(fleet, -1, width),
            dw_down.astype(BF).reshape(fleet, -1, width),
        ],
        axis=1,
    )
    dense_grads = lax.psum_scatter(dense_grads, ("dp", "seq"), scatter_dimension=0)

    grad_heads = dot_t(grad_attn, w_output).astype(BF)
    pad = ((0, 0), (0, lanes - real))
    grad_heads = [
        jnp.pad(grad_heads[:, j * real : (j + 1) * real], pad) for j in range(team)
    ]
    grad_heads = jnp.concatenate(hand_out(grad_heads, team), axis=0)
    grad_qkv = attention_backward(slots, live, qkv, grad_heads, log_total, segcol, segrow)
    dw_qkv = t_dot(all_tokens, grad_qkv)
    db_qkv = jnp.sum(grad_qkv.astype(F32), axis=0)
    back = dot_t(grad_qkv, w_qkv).reshape(team, -1, width)
    back = [back[0]] + [part.astype(BF) for part in back[1:]]
    back = hand_out(back, team)
    token_grad = grad_resid
    for part in back:
        token_grad = token_grad + part.astype(F32)
    token_grad = from_plane(token_grad.astype(BF), local, sub, team, core)

    def widen(array):
        full = jnp.zeros(array.shape[:-1] + (width,), array.dtype)
        return lax.dynamic_update_slice_in_dim(full, array[..., :real], rank * real, array.ndim - 1)

    dws = [
        widen(dw_qkv[:, i * lanes : (i + 1) * lanes].astype(BF)).reshape(fleet, share, width)
        for i in range(3)
    ]
    db_query, db_value = widen(db_qkv[:lanes]), widen(db_qkv[2 * lanes :])
    smalls = [db_query, db_value, db_output, dg_first, db_first, db_down, dg_second, db_second]
    smalls = jnp.concatenate(
        [v.reshape(fleet, share) for v in smalls] + [db_hidden.reshape(fleet, share_hidden)], axis=1
    ).astype(BF)
    smalls = jnp.pad(smalls, ((0, 0), (0, 8 * width - smalls.shape[1]))).reshape(fleet, 8, width)
    first_grads = jnp.concatenate(dws + [smalls], axis=1)
    first_grads = lax.psum_scatter(first_grads, ("dp", "seq"), scatter_dimension=0)

    dense_grads, first_grads = dense_grads.astype(F32), first_grads.astype(F32)
    dw_query, dw_key, dw_value = (first_grads[i * share : (i + 1) * share] for i in range(3))
    line = first_grads[3 * share]
    vectors = [line[i * share : (i + 1) * share] for i in range(8)]
    db_query, db_value, db_output, dg_first, db_first, db_down, dg_second, db_second = vectors
    return (
        result,
        token_grad,
        dw_query,
        db_query,
        dw_key,
        dw_value,
        db_value,
        dense_grads[:share],
        db_output,
        dg_first,
        db_first,
        dense_grads[share:cut].reshape(share, hidden),
        line[8 * share : 8 * share + share_hidden],
        dense_grads[cut:],
        db_down,
        dg_second,
        db_second,
    )


def solution(mesh):
    in_specs = (
        P("dp", "seq", None),
        P("dp", None),
        P("dp"),
        P("dp", None, None),
        P(("dp", "seq"), None),
        P(("dp", "seq")),
        P(("dp", "seq"), None),
        P(("dp", "seq"), None),
        P(("dp", "seq")),
        P(("dp", "seq"), None),
        P(("dp", "seq")),
        P(("dp", "seq")),
        P(("dp", "seq")),
        P(("dp", "seq"), None),
        P(("dp", "seq")),
        P(("dp", "seq"), None),
        P(("dp", "seq")),
        P(("dp", "seq")),
        P(("dp", "seq")),
        P("dp", "seq", None),
    )
    out_specs = (
        P("dp", "seq", None),
        P("dp", "seq", None),
        P(("dp", "seq"), None),
        P(("dp", "seq")),
        P(("dp", "seq"), None),
        P(("dp", "seq"), None),
        P(("dp", "seq")),
        P(("dp", "seq"), None),
        P(("dp", "seq")),
        P(("dp", "seq")),
        P(("dp", "seq")),
        P(("dp", "seq"), None),
        P(("dp", "seq")),
        P(("dp", "seq"), None),
        P(("dp", "seq")),
        P(("dp", "seq")),
        P(("dp", "seq")),
    )
    return jax.shard_map(
        per_device, mesh=mesh, in_specs=in_specs, out_specs=out_specs, check_vma=False
    )
```
